32 devices in a mesh: shift: 4 (over z), dom: 8 (over y, x, core).
Axes of the slice: x: 2, y: 2, z: 4, core: 2. Of those that a mesh axis runs over, the one named last changes fastest.
Arguments:
- excitation: float32 [128, 8192], P('shift', 'dom'), may hold values from -6 to 6
- g_diagonal: float32 [64, 128, 128], P('dom'), may hold values from -3 to 13
- g_coupling: float32 [64, 4, 128, 128], P('dom'), may hold values from -3.1 to 3.1
- c_blocks: float32 [64, 128, 128], P('dom'), may hold values from -0.5 to 2.5
- shifts: float32 [4], P('shift'), may hold values from 0.05 to 5
- jacobi_inverse: bfloat16 [4, 64, 128, 128], P('shift', 'dom'), may hold values from -3 to 3, as said below
- tile_source: int32 [64, 4], P('dom'), may hold values from 0 to 11, as said below
- send_list: int32 [8, 2, 2], P('dom'), may hold values from -1 to 7, as said below
- sweep_limits: int32 [4], P('shift'), may hold values from 1 to 4
Outputs:
- basis: float32 [128, 8192], P('shift', 'dom')
- reduced_g: float32 [128, 128], P('shift')
- reduced_c: float32 [128, 128], P('shift')
The draws below stay inside these ranges and needn't reach their ends.
Inputs may be any that keep to these rules, and one draw needn't show every extreme that they name: jacobi_inverse[s, i] is the inverse of g_diagonal[i] + shifts[s] c_blocks[i], rounded to bfloat16. `tile_source`: A slot below 2 names a live entry of the left neighbour's list send_list[d-1, 1], a slot of 10 or more a live entry of the right neighbour's list send_list[d+1, 0], the others a local block; the first partition uses no left slot, the last no right slot. `send_list`: each list holds one to 2 live local block numbers followed by -1 padding.
All inputs are finite; a program needn't handle non-finite values.
Results may differ from the reference program's by a relative error of at most 0.0024.
Values sent between devices are 32-bit elements; how exact they have to be, the bound alone decides.
A program may use at most 64 MiB of HBM per device.

```python
import math
import jax
import jax.numpy as jnp
from jax import lax

PORTS = 32
BLOCK = 128
TILES = 4
EXPORT = 2
SWEEPS = 4
BLK_DEV = 8
NPART = 8
SHIFTS = 4
COLS = 128
NODES = 8192


def float_parts(key):
    base_key = jax.random.fold_in(key, 7)
    subkeys = jax.random.split(base_key, 6)
    blocks_all = BLK_DEV * NPART
    node_scale = jnp.exp(jax.random.uniform(subkeys[0], (blocks_all, BLOCK), minval=0.0, maxval=math.log(10.0)))
    root = jnp.sqrt(node_scale)
    mixing = jnp.clip(jax.random.normal(subkeys[1], (blocks_all, BLOCK, BLOCK)), -4.0, 4.0) * (0.25 / math.sqrt(BLOCK))
    identity = jnp.eye(BLOCK, dtype=jnp.float32)
    g_diagonal = identity * node_scale[:, :, None] + mixing * root[:, :, None] * root[:, None, :]
    coupling = jnp.clip(jax.random.normal(subkeys[2], (blocks_all, TILES, BLOCK, BLOCK)), -4.0, 4.0)
    g_coupling = coupling * (0.3 / math.sqrt(BLOCK)) * node_scale[:, None, :, None]
    cap_scale = jnp.exp(jax.random.uniform(subkeys[3], (blocks_all, BLOCK), minval=math.log(0.5), maxval=math.log(2.0)))
    cap_root = jnp.sqrt(cap_scale)
    cap_mix = jnp.clip(jax.random.normal(subkeys[4], (blocks_all, BLOCK, BLOCK)), -4.0, 4.0) * (0.15 / math.sqrt(BLOCK))
    c_blocks = identity * cap_scale[:, :, None] + cap_mix * cap_root[:, :, None] * cap_root[:, None, :]
    shifts = jnp.exp(jax.random.uniform(subkeys[5], (SHIFTS,), minval=math.log(0.05), maxval=math.log(5.0)))
    system = g_diagonal[None] + shifts[:, None, None, None] * c_blocks[None]
    inverse = jnp.linalg.inv(system)
    return (g_diagonal, g_coupling, c_blocks, shifts, inverse)


def graph_parts(key):
    base_key = jax.random.fold_in(key, 3)
    subkeys = jax.random.split(base_key, 7)
    blocks_all = BLK_DEV * NPART
    counts = jax.random.randint(subkeys[0], (NPART, 2), 1, EXPORT + 1)
    chosen = jax.random.randint(subkeys[1], (), 0, NPART - 1)
    sparse_part = (chosen + 2) % NPART
    counts = counts.at[chosen, 1].set(EXPORT).at[chosen + 1, 0].set(EXPORT).at[sparse_part, 0].set(1)
    entries = jax.random.randint(subkeys[2], (NPART, 2, EXPORT), 0, BLK_DEV)
    entries = entries.at[chosen, 1, 0].set(BLK_DEV - 1)
    slots = jnp.arange(EXPORT, dtype=jnp.int32)
    send_list = jnp.where(slots[None, None, :] < counts[:, :, None], entries, -1)
    owner = jnp.arange(blocks_all, dtype=jnp.int32) // BLK_DEV
    kinds = jax.random.randint(subkeys[3], (blocks_all, TILES), 0, 3)
    raw_pick = jax.random.randint(subkeys[4], (blocks_all, TILES), 0, 1 << 20)
    left_count = counts[jnp.maximum(owner - 1, 0), 1]
    right_count = counts[jnp.minimum(owner + 1, NPART - 1), 0]
    local_slot = EXPORT + raw_pick % BLK_DEV
    left_slot = raw_pick % left_count[:, None]
    right_slot = EXPORT + BLK_DEV + raw_pick % right_count[:, None]
    has_left = (owner > 0)[:, None]
    has_right = (owner < NPART - 1)[:, None]
    sources = jnp.where((kinds == 1) & has_left, left_slot, jnp.where((kinds == 2) & has_right, right_slot, local_slot))
    sources = sources.at[chosen * BLK_DEV + BLK_DEV - 1, 0].set(2 * EXPORT + BLK_DEV - 1)
    sources = sources.at[(chosen + 1) * BLK_DEV, 0].set(0)
    limits = jax.random.randint(subkeys[5], (SHIFTS,), 1, SWEEPS + 1)
    longest = jax.random.randint(subkeys[6], (), 0, SHIFTS)
    limits = limits.at[longest].set(SWEEPS).at[(longest + 1) % SHIFTS].set(1)
    return (sources.astype(jnp.int32), send_list.astype(jnp.int32), limits.astype(jnp.int32))


def draw_g_diagonal(key, part):
    return float_parts(key)[0]


def draw_g_coupling(key, part):
    return float_parts(key)[1]


def draw_c_blocks(key, part):
    return float_parts(key)[2]


def draw_shifts(key, part):
    return float_parts(key)[3]


def draw_jacobi_inverse(key, part):
    return float_parts(key)[4].astype(jnp.bfloat16)


def draw_tile_source(key, part):
    return graph_parts(key)[0]


def draw_send_list(key, part):
    return graph_parts(key)[1]


def draw_sweep_limits(key, part):
    return graph_parts(key)[2]


def level_of(key, dims, pieces, least, largest):
    gain = 1.0
    for position, parts in pieces:
        heights = jax.random.uniform(jax.random.fold_in(jax.random.fold_in(key, 6), position), (parts,), jnp.float32, least / len(pieces), largest / len(pieces))
        gain = gain * jnp.repeat(jnp.exp(heights), dims[position] // parts).reshape((-1,) + (1,) * (len(dims) - 1 - position))
    return gain


def scatter_about(key, extent, width, bound, pieces=(), kind=jnp.bfloat16):
    values = jax.random.normal(key, extent, jnp.float32) * width
    if len(pieces) > 0:
        values = level_of(key, extent, pieces, -0.22, 0.18) * values
    return jnp.clip(values, min=-bound, max=bound).astype(kind)


def setup_inputs(seed: int = 0) -> dict:
    streams_of = jax.random.split(jax.random.key(seed), 10)
    excitation = scatter_about(streams_of[0], (COLS, NODES), 1.0, 6.0, ((0, 4), (1, 8)), jnp.float32)
    g_diagonal = draw_g_diagonal(jax.random.fold_in(streams_of[9], 71), 0)
    g_coupling = draw_g_coupling(jax.random.fold_in(streams_of[9], 71), 0)
    c_blocks = draw_c_blocks(jax.random.fold_in(streams_of[9], 71), 0)
    shifts = draw_shifts(jax.random.fold_in(streams_of[9], 71), 0)
    jacobi_inverse = draw_jacobi_inverse(jax.random.fold_in(streams_of[9], 71), 0)
    tile_source = draw_tile_source(jax.random.fold_in(streams_of[9], 71), 0)
    send_list = draw_send_list(jax.random.fold_in(streams_of[9], 71), 0)
    sweep_limits = draw_sweep_limits(jax.random.fold_in(streams_of[9], 71), 0)
    return {"excitation": excitation, "g_diagonal": g_diagonal, "g_coupling": g_coupling, "c_blocks": c_blocks, "shifts": shifts, "jacobi_inverse": jacobi_inverse, "tile_source": tile_source, "send_list": send_list, "sweep_limits": sweep_limits}


def extend(field, send_list):
    columns = field.shape[0]
    picker = (send_list[..., None] == jnp.arange(BLK_DEV, dtype=jnp.int32)).astype(jnp.float32)
    outgoing = jnp.einsum('dsjb,pdbc->pdsjc', picker, field, precision=lax.Precision.HIGHEST)
    nothing = jnp.zeros((columns, 1, EXPORT, BLOCK), jnp.float32)
    from_left = jnp.concatenate([nothing, outgoing[:, :-1, 1]], axis=1)
    from_right = jnp.concatenate([outgoing[:, 1:, 0], nothing], axis=1)
    return jnp.concatenate([from_left, field, from_right], axis=2)

def apply_both(field, g_diagonal, g_coupling, c_blocks, tile_source, send_list):
    columns = field.shape[0]
    extended = extend(field, send_list)
    sources = tile_source.reshape(NPART, BLK_DEV * TILES)
    chooser = (sources[..., None] == jnp.arange(BLK_DEV + 2 * EXPORT, dtype=jnp.int32)).astype(jnp.float32)
    picked = jnp.einsum('due,pdec->pduc', chooser, extended, precision=lax.Precision.HIGHEST)
    picked = picked.reshape(columns, NPART, BLK_DEV, TILES, BLOCK)
    diagonal = g_diagonal.reshape(NPART, BLK_DEV, BLOCK, BLOCK)
    coupling = g_coupling.reshape(NPART, BLK_DEV, TILES, BLOCK, BLOCK)
    capacity = c_blocks.reshape(NPART, BLK_DEV, BLOCK, BLOCK)
    g_image = jnp.einsum('dbrc,pdbc->pdbr', diagonal, field, precision=lax.Precision.HIGHEST)
    g_image = g_image + jnp.einsum('dbkrc,pdbkc->pdbr', coupling, picked, precision=lax.Precision.HIGHEST)
    c_image = jnp.einsum('dbrc,pdbc->pdbr', capacity, field, precision=lax.Precision.HIGHEST)
    return (g_image, c_image)

def reference(excitation, g_diagonal, g_coupling, c_blocks, shifts, jacobi_inverse, tile_source, send_list, sweep_limits):
    right_sides = excitation.reshape(SHIFTS, PORTS, NPART, BLK_DEV, BLOCK)

    def solve_one(items):
        rhs_one, shift_value, limit, inverse = items
        inverse = inverse.astype(jnp.float32).reshape(NPART, BLK_DEV, BLOCK, BLOCK)
        iterate = jnp.zeros_like(rhs_one)
        for sweep_index in range(SWEEPS):
            if sweep_index == 0:
                residual = rhs_one
            else:
                g_image, c_image = apply_both(iterate, g_diagonal, g_coupling, c_blocks, tile_source, send_list)
                residual = rhs_one - (g_image + shift_value * c_image)
            rounded = lax.optimization_barrier(residual.astype(jnp.bfloat16)).astype(jnp.float32)
            correction = jnp.einsum('dbrc,pdbc->pdbr', inverse, rounded, precision=lax.Precision.HIGHEST)
            iterate = jnp.where(sweep_index < limit, iterate + correction, iterate)
        return iterate
    solved = lax.map(solve_one, (right_sides, shifts, sweep_limits, jacobi_inverse))
    raw = solved.reshape(COLS, NODES)
    gram = jnp.dot(raw, raw.T, precision=lax.Precision.HIGHEST) / NODES
    factor = jnp.linalg.cholesky(gram)
    inverse_factor = lax.linalg.triangular_solve(factor, jnp.eye(COLS, dtype=jnp.float32), left_side=True, lower=True)
    basis = jnp.dot(inverse_factor, raw, precision=lax.Precision.HIGHEST)
    g_image, c_image = apply_both(basis.reshape(COLS, NPART, BLK_DEV, BLOCK), g_diagonal, g_coupling, c_blocks, tile_source, send_list)
    reduced_g = jnp.dot(g_image.reshape(COLS, NODES), basis.T, precision=lax.Precision.HIGHEST) / NODES
    reduced_c = jnp.dot(c_image.reshape(COLS, NODES), basis.T, precision=lax.Precision.HIGHEST) / NODES
    return (basis, reduced_g, reduced_c)
```

```python
import functools

import jax
import jax.numpy as jnp
from jax import lax
from jax.experimental import pallas as pl
from jax.experimental.pallas import tpu as pltpu
from jax.sharding import PartitionSpec as P

SWEEPS = 4
PANEL = 128
GROUP = 8
MESH = pl.DeviceIdType.MESH
HIGHEST = lax.Precision.HIGHEST


def split(value):
    high = value.astype(jnp.bfloat16)
    low = (value - high.astype(jnp.float32)).astype(jnp.bfloat16)
    return high, low


def across(a, b, precision=None):
    return lax.dot_general(
        a, b, (((1,), (1,)), ((), ())), precision=precision, preferred_element_type=jnp.float32
    )


def folded(product, rows, width):
    return (product[rows:, width:] + (product[rows:, :width] + product[:rows, width:])) + product[
        :rows, :width
    ]


def panel_inverse(block):
    size = block.shape[0]
    wide = 2 * size
    lanes = lax.broadcasted_iota(jnp.int32, (size, size), 1)
    rows = lax.broadcasted_iota(jnp.int32, (size, size), 0)
    eye = (lanes == rows).astype(jnp.float32)
    work = jnp.concatenate([block, eye], axis=1)
    tiles = [work[8 * t : 8 * t + 8] for t in range(size // 8)]
    sub = lax.broadcasted_iota(jnp.int32, (8, wide), 0)
    group = range(GROUP)

    def along(value):
        return jnp.concatenate([value] * (wide // 128), axis=1)

    for k in range(0, size, GROUP):
        home, at = k // 8, k % 8
        live = range(home if at + GROUP < 8 else home + 1, size // 8)

        def columns_of(t):
            return [jnp.broadcast_to(tiles[t][:, k + j : k + j + 1], (8, 128)) for j in group]

        home_columns = columns_of(home)
        entry = {
            (i, j): jnp.broadcast_to(home_columns[j][at + i : at + i + 1], (8, 128))
            for j in group
            for i in range(j, GROUP)
        }
        ratio, inverse = {}, []
        for j in group:
            inverse.append(1.0 / entry[j, j])
            for i in range(j + 1, GROUP):
                ratio[i, j] = entry[i, j] * inverse[j]
            for m in range(j + 1, GROUP):
                for i in range(m, GROUP):
                    entry[i, m] = entry[i, m] - ratio[i, j] * entry[m, j]
        ratio = {at_pair: along(value) for at_pair, value in ratio.items()}
        lines = [jnp.broadcast_to(tiles[home][at + j : at + j + 1], (8, wide)) for j in group]
        for j in group:
            for i in range(j + 1, GROUP):
                lines[i] = lines[i] - ratio[i, j] * lines[j]
        solved = [along(inverse[j]) * lines[j] for j in group]
        for j in reversed(group):
            for m in range(j):
                solved[m] = solved[m] - ratio[j, m] * solved[j]
        for t in live:
            columns = home_columns if t == home else columns_of(t)
            change = along(columns[0]) * solved[0]
            for j in range(1, GROUP):
                change = change + along(columns[j]) * solved[j]
            new = tiles[t] - change
            tiles[t] = jnp.where(sub >= at + GROUP, new, tiles[t]) if t == home else new
        for j in range(1, GROUP):
            tiles[home] = jnp.where(sub == at + j, lines[j], tiles[home])
    work = jnp.concatenate(tiles, axis=0)
    wide_lane = lax.broadcasted_iota(jnp.int32, work.shape, 1)
    wide_row = lax.broadcasted_iota(jnp.int32, work.shape, 0)
    pivots = jnp.sum(jnp.where(wide_lane == wide_row, work, 0.0), axis=1, keepdims=True)
    return (work * lax.rsqrt(pivots))[:, size:]


def inverse_of_factor(gram):
    total = gram.shape[0]
    if total <= PANEL:
        return panel_inverse(gram)
    rows = lax.broadcasted_iota(jnp.int32, (total, total), 0)
    lanes = lax.broadcasted_iota(jnp.int32, (total, total), 1)
    work = jnp.concatenate([gram, (rows == lanes).astype(jnp.float32)], axis=1)
    found = []
    for first in range(0, total, PANEL):
        small = panel_inverse(work[:PANEL, first : first + PANEL])
        panel = jnp.dot(small, work[:PANEL], precision=HIGHEST, preferred_element_type=jnp.float32)
        found.append(panel[:, total:])
        if first + PANEL < total:
            left = panel[:, first + PANEL : total]
            work = work[PANEL:] - lax.dot_general(
                left,
                panel,
                (((0,), (0,)), ((), ())),
                precision=HIGHEST,
                preferred_element_type=jnp.float32,
            )
    return jnp.concatenate(found, axis=0)


def kernel(
    shift_count,
    dom_count,
    right_hbm,
    diag_hbm,
    coupling_hbm,
    cap_hbm,
    shift_ref,
    inverse_hbm,
    source_hbm,
    list_hbm,
    limit_ref,
    basis_ref,
    red_g_ref,
    red_c_ref,
    source_ref,
    list_ref,
    right_ref,
    diag_ref,
    coupling_ref,
    cap_ref,
    inverse_ref,
    own_w,
    near_w,
    cap_w,
    field,
    parts,
    outgoing,
    incoming,
    raw_all,
    product,
    scattered,
    summed,
    reduced,
    factor_ref,
    load_sems,
    halo_send,
    halo_recv,
    gather_send,
    gather_recv,
    scatter_send,
    scatter_recv,
    sum_send,
    sum_recv,
    red_send,
    red_recv,
):
    me_s = lax.axis_index("shift")
    me_d = lax.axis_index("dom")
    blocks, width, _ = diag_ref.shape
    tile_count = coupling_ref.shape[1]
    ports = right_ref.shape[0]
    spread = outgoing.shape[2]
    total = shift_count * ports
    node_count = blocks * width * dom_count

    loads = []
    pairs = (
        (inverse_hbm, inverse_ref),
        (right_hbm, right_ref),
        (diag_hbm, diag_ref),
        (cap_hbm, cap_ref),
        (coupling_hbm, coupling_ref),
        (list_hbm, list_ref),
        (source_hbm, source_ref),
    )
    for slot, (source, target) in enumerate(pairs):
        load = pltpu.make_async_copy(source, target, load_sems.at[slot])
        load.start()
        loads.append(load)

    barrier = pltpu.get_barrier_semaphore()
    for o in range(1, dom_count):
        pl.semaphore_signal(
            barrier, inc=1, device_id=(me_s, lax.rem(me_d + o, dom_count)), device_id_type=MESH
        )
    for o in range(1, shift_count):
        pl.semaphore_signal(
            barrier, inc=1, device_id=(lax.rem(me_s + o, shift_count), me_d), device_id_type=MESH
        )


    def halo_copy(step, side):
        target = me_d - 1 if side == 0 else me_d + 1
        return pltpu.make_async_remote_copy(
            src_ref=outgoing.at[step, side],
            dst_ref=incoming.at[step, 1 - side],
            send_sem=halo_send.at[step, side],
            recv_sem=halo_recv.at[step, 1 - side],
            device_id=(me_s, target),
            device_id_type=MESH,
        )

    def halo_arrival(step, side):
        return pltpu.make_async_remote_copy(
            src_ref=outgoing.at[step, 1 - side],
            dst_ref=incoming.at[step, side],
            send_sem=halo_send.at[step, 1 - side],
            recv_sem=halo_recv.at[step, side],
            device_id=(me_s, me_d - 1 if side == 0 else me_d + 1),
            device_id_type=MESH,
        )

    def there(side):
        return me_d > 0 if side == 0 else me_d < dom_count - 1

    def send_halo(step):
        for side in range(2):
            for j in range(spread):
                outgoing[step, side, j] = field[step, jnp.maximum(list_ref[0, side, j], 0)]

            @pl.when(there(side))
            def _():
                halo_copy(step, side).start()

    def take_halo(step):
        for side in range(2):

            @pl.when(there(side))
            def _():
                halo_arrival(step, side).wait_recv()

            base = 0 if side == 0 else spread + blocks
            for j in range(spread):
                high, low = split(incoming[step, side, j])
                parts[step, base + j, :ports] = high
                parts[step, base + j, ports:] = low

    def store_field(step, b, value):
        field[step, b] = value
        high, low = split(value)
        parts[step, spread + b, :ports] = high
        parts[step, spread + b, ports:] = low

    def own_image(step, b):
        return folded(across(parts[step, spread + b], own_w[b]), ports, width)

    def near_image(step, b):
        picked = jnp.concatenate(
            [parts[step, source_ref[k, b]] for k in range(tile_count)], axis=1
        )
        return folded(across(picked, near_w[b]), ports, width)

    def column(b):
        return slice(b * width, (b + 1) * width)

    for slot in (0, 1, 5):
        loads[slot].wait()
    limit = limit_ref[0]
    for b in range(blocks):
        rounded = right_ref[:, column(b)].astype(jnp.bfloat16)
        correction = across(rounded, inverse_ref[0, b])
        store_field(0, b, jnp.where(limit > 0, correction, jnp.zeros_like(correction)))
    for side in range(2):

        @pl.when(jnp.logical_not(there(side)))
        def _():
            for step in range(SWEEPS):
                for j in range(spread):
                    incoming[step, side, j] = jnp.zeros((ports, width), jnp.float32)

    pl.semaphore_wait(barrier, dom_count + shift_count - 2)
    send_halo(0)

    for slot in (2, 3, 6):
        loads[slot].wait()
    shift_value = shift_ref[0]
    for b in range(blocks):
        high, low = split(diag_ref[b] + shift_value * cap_ref[b])
        own_w[b, :width] = high
        own_w[b, width:] = low
        high, low = split(cap_ref[b])
        cap_w[b, :width] = high
        cap_w[b, width:] = low
    loads[4].wait()
    for b in range(blocks):
        for k in range(tile_count):
            high, low = split(coupling_ref[b, k])
            near_w[b, :width, column(k)] = high
            near_w[b, width:, column(k)] = low

    for sweep in range(1, SWEEPS):
        own = [own_image(sweep - 1, b) for b in range(blocks)]
        take_halo(sweep - 1)
        fresh = []
        for b in range(blocks):
            residual = right_ref[:, column(b)] - (own[b] + near_image(sweep - 1, b))
            correction = across(residual.astype(jnp.bfloat16), inverse_ref[0, b])
            before = field[sweep - 1, b]
            fresh.append(jnp.where(sweep < limit, before + correction, before))
        for b in range(blocks):
            store_field(sweep, b, fresh[b])
        send_halo(sweep)

    for b in range(blocks):
        raw_all[me_s, :, column(b)] = field[SWEEPS - 1, b]
    gathers = []
    for o in range(1, shift_count):
        copy = pltpu.make_async_remote_copy(
            src_ref=raw_all.at[me_s],
            dst_ref=raw_all.at[me_s],
            send_sem=gather_send.at[o],
            recv_sem=gather_recv.at[o],
            device_id=(lax.rem(me_s + o, shift_count), me_d),
            device_id_type=MESH,
        )
        copy.start()
        gathers.append(copy)

    final = SWEEPS - 1
    own = [own_image(final, b) for b in range(blocks)]
    cap = [folded(across(parts[final, spread + b], cap_w[b]), ports, width) for b in range(blocks)]
    take_halo(SWEEPS - 1)
    images = [own[b] + near_image(final, b) - shift_value * cap[b] for b in range(blocks)]
    both = jnp.concatenate(
        [jnp.concatenate(images, axis=1), jnp.concatenate(cap, axis=1)], axis=0
    )
    for copy in gathers:
        copy.wait()
    everything = raw_all[...].reshape(total, blocks * width)
    scale = 1.0 / node_count
    gram_part = across(everything, everything, HIGHEST) * scale
    both_part = across(both, everything, HIGHEST) * scale
    gram_rows = total // dom_count
    both_rows = 2 * ports // dom_count
    for j in range(dom_count):
        product[j, :gram_rows] = gram_part[j * gram_rows : (j + 1) * gram_rows]
        product[j, gram_rows:] = both_part[j * both_rows : (j + 1) * both_rows]

    scatters = []
    for o in range(1, dom_count):
        target = lax.rem(me_d + o, dom_count)
        copy = pltpu.make_async_remote_copy(
            src_ref=product.at[target],
            dst_ref=scattered.at[o],
            send_sem=scatter_send.at[o],
            recv_sem=scatter_recv.at[o],
            device_id=(me_s, target),
            device_id_type=MESH,
        )
        copy.start()
        scatters.append(copy)
    mine = product[me_d]
    for o, copy in enumerate(scatters):
        copy.wait()
        mine = mine + scattered[o + 1]
    summed[me_d] = mine
    sums = []
    for o in range(1, dom_count):
        copy = pltpu.make_async_remote_copy(
            src_ref=summed.at[me_d],
            dst_ref=summed.at[me_d],
            send_sem=sum_send.at[o],
            recv_sem=sum_recv.at[o],
            device_id=(me_s, lax.rem(me_d + o, dom_count)),
            device_id_type=MESH,
        )
        copy.start()
        sums.append(copy)
    for copy in sums:
        copy.wait()

    reduced[me_s] = jnp.concatenate([summed[j, gram_rows:] for j in range(dom_count)], axis=0)
    last = []
    for o in range(1, shift_count):
        copy = pltpu.make_async_remote_copy(
            src_ref=reduced.at[me_s],
            dst_ref=reduced.at[me_s],
            send_sem=red_send.at[o],
            recv_sem=red_recv.at[o],
            device_id=(lax.rem(me_s + o, shift_count), me_d),
            device_id_type=MESH,
        )
        copy.start()
        last.append(copy)

    gram = jnp.concatenate([summed[j, :gram_rows] for j in range(dom_count)], axis=0)
    factor_ref[...] = inverse_of_factor(gram)
    own_rows = factor_ref[pl.ds(pl.multiple_of(me_s * ports, ports), ports), :]
    basis_ref[...] = jnp.dot(
        own_rows, everything, precision=HIGHEST, preferred_element_type=jnp.float32
    )
    for copy in last:
        copy.wait()
    inverse_factor = factor_ref[...]
    for half, ref in ((0, red_g_ref), (1, red_c_ref)):
        middle = jnp.concatenate(
            [reduced[t, half * ports : (half + 1) * ports] for t in range(shift_count)], axis=0
        )
        left = jnp.dot(own_rows, middle, precision=HIGHEST, preferred_element_type=jnp.float32)
        ref[...] = across(left, inverse_factor, HIGHEST)
    for step in range(SWEEPS):
        for side in range(2):

            @pl.when(there(side))
            def _():
                halo_copy(step, side).wait_send()


def local(
    excitation,
    g_diagonal,
    g_coupling,
    c_blocks,
    shifts,
    jacobi_inverse,
    tile_source,
    send_list,
    sweep_limits,
):
    shift_count = lax.axis_size("shift")
    dom_count = lax.axis_size("dom")
    ports, nodes = excitation.shape
    blocks, width, _ = g_diagonal.shape
    tile_count = g_coupling.shape[1]
    spread = send_list.shape[2]
    total = ports * shift_count
    chunk = total // dom_count + 2 * ports // dom_count
    f32, bf16 = jnp.float32, jnp.bfloat16
    anywhere = pl.BlockSpec(memory_space=pltpu.HBM)
    vector = pl.BlockSpec(memory_space=pltpu.VMEM)
    scalar = pl.BlockSpec(memory_space=pltpu.SMEM)
    dma = pltpu.SemaphoreType.DMA
    results = pl.pallas_call(
        functools.partial(kernel, shift_count, dom_count),
        out_shape=(
            pltpu.VMEM((ports, nodes), f32),
            pltpu.VMEM((ports, total), f32),
            pltpu.VMEM((ports, total), f32),
        ),
        in_specs=[
            anywhere,
            anywhere,
            anywhere,
            anywhere,
            scalar,
            anywhere,
            anywhere,
            anywhere,
            scalar,
        ],
        out_specs=(vector, vector, vector),
        scratch_shapes=[
            pltpu.SMEM(tile_source.shape[::-1], jnp.int32),
            pltpu.SMEM(send_list.shape, jnp.int32),
            pltpu.VMEM(excitation.shape, f32),
            pltpu.VMEM(g_diagonal.shape, f32),
            pltpu.VMEM(g_coupling.shape, f32),
            pltpu.VMEM(c_blocks.shape, f32),
            pltpu.VMEM(jacobi_inverse.shape, bf16),
            pltpu.VMEM((blocks, 2 * width, width), bf16),
            pltpu.VMEM((blocks, 2 * width, tile_count * width), bf16),
            pltpu.VMEM((blocks, 2 * width, width), bf16),
            pltpu.VMEM((SWEEPS, blocks, ports, width), f32),
            pltpu.VMEM((SWEEPS, blocks + 2 * spread, 2 * ports, width), bf16),
            pltpu.VMEM((SWEEPS, 2, spread, ports, width), f32),
            pltpu.VMEM((SWEEPS, 2, spread, ports, width), f32),
            pltpu.VMEM((shift_count, ports, nodes), f32),
            pltpu.VMEM((dom_count, chunk, total), f32),
            pltpu.VMEM((dom_count, chunk, total), f32),
            pltpu.VMEM((dom_count, chunk, total), f32),
            pltpu.VMEM((shift_count, 2 * ports, total), f32),
            pltpu.VMEM((total, total), f32),
            dma((7,)),
            dma((SWEEPS, 2)),
            dma((SWEEPS, 2)),
            dma((shift_count,)),
            dma((shift_count,)),
            dma((dom_count,)),
            dma((dom_count,)),
            dma((dom_count,)),
            dma((dom_count,)),
            dma((shift_count,)),
            dma((shift_count,)),
        ],
        compiler_params=pltpu.CompilerParams(
            collective_id=0, has_side_effects=True, vmem_limit_bytes=60 * 1024 * 1024
        ),
    )(
        excitation,
        g_diagonal,
        g_coupling,
        c_blocks,
        shifts,
        jacobi_inverse,
        tile_source.T,
        send_list,
        sweep_limits,
    )
    results = [pltpu.with_memory_space_constraint(r, pltpu.VMEM) for r in results]
    return pl.pallas_call(
        deliver,
        out_shape=(
            jax.ShapeDtypeStruct((ports, nodes), f32),
            jax.ShapeDtypeStruct((ports, total), f32),
            jax.ShapeDtypeStruct((ports, total), f32),
        ),
        in_specs=[vector] * 3,
        out_specs=(anywhere,) * 3,
        scratch_shapes=[dma((3,))],
    )(*results)


def deliver(*refs):
    sems = refs[-1]
    copies = [pltpu.make_async_copy(refs[i], refs[i + 3], sems.at[i]) for i in range(3)]
    for copy in copies:
        copy.start()
    for copy in copies:
        copy.wait()


def solution(mesh):
    return jax.shard_map(
        local,
        mesh=mesh,
        in_specs=(
            P("shift", "dom"),
            P("dom", None, None),
            P("dom", None, None, None),
            P("dom", None, None),
            P("shift"),
            P("shift", "dom", None, None),
            P("dom", None),
            P("dom", None, None),
            P("shift"),
        ),
        out_specs=(P("shift", "dom"), P("shift", None), P("shift", None)),
        check_vma=False,
    )
```
